32 devices in a mesh: feat: 8 (over z, y), tok: 4 (over x, core).
Axes of the slice: x: 2, y: 2, z: 4, core: 2. Of those that a mesh axis runs over, the one named last changes fastest.
Arguments:
- activations: bfloat16 [2048, 7168], P('tok', 'feat'), may hold values from -6 to 6
- top_lists: int32 [2048, 64], P('tok'), may hold values from 0 to 4095, all different within a row
- encoder_weight: bfloat16 [7168, 4096], P(None, 'feat'), may hold values from -0.0625 to 0.0625
- encoder_bias: float32 [4096], P('feat'), may hold values from -3 to 3
- decoder_weight: bfloat16 [7168, 4096], P(None, 'feat'), may hold values from -0.125 to 0.125
- decoder_bias: float32 [7168], replicated, may hold values from -3 to 3
Outputs:
- encoder_grad: float32 [7168, 4096], P('tok', 'feat')
- decoder_grad: float32 [7168, 4096], P('tok', 'feat')
The draws below stay inside these ranges and needn't reach their ends.
All inputs are finite; a program needn't handle non-finite values.
Results may differ from the reference program's by a relative error of at most 0.004.
Values may be sent and summed in bfloat16 or wider, within the bound.
A program may use at most 128 MiB of HBM per device.

```python
import jax
import jax.numpy as jnp
from jax import lax

D = 3584
TOPK = 64
FEATURES = 4096
TOKENS = 2048


def block_levels(own_key, dims, cuts, low, top_value):
    level, own = 1.0, jax.random.fold_in(own_key, 6)
    for position, shards_of in cuts:
        steps = jnp.exp(jax.random.uniform(jax.random.fold_in(own, position), (shards_of,), jnp.float32, low / len(cuts), top_value / len(cuts)))
        level = level * jnp.repeat(steps, dims[position] // shards_of).reshape([-1 if axis == position else 1 for axis in range(len(dims))])
    return level


def distinct(stream_key, rows, number_of, top, lift):
    sequence = jax.random.permutation(jax.random.fold_in(stream_key, 1), number_of)
    favour = sequence
    for power in range(3):
        favour = favour * favour // number_of
    favour = favour * lift // number_of
    lots = jax.random.randint(jax.random.fold_in(stream_key, 2), (rows, number_of), 0, 4096) + favour
    sure = jax.random.permutation(jax.random.fold_in(stream_key, 3), rows)[jnp.arange(number_of) % rows]
    lots = jnp.where(jnp.arange(rows)[:, None] == sure[None, :], 1 << 14, lots)
    merit = lots * number_of + jnp.arange(number_of)
    return lax.top_k(merit.astype(jnp.int32), top)[1].astype(jnp.int32)


def gaussian(rng, extent, deviation, most, cuts=(), kind=jnp.bfloat16):
    entries = jax.random.normal(rng, extent, jnp.float32) * deviation
    if len(cuts) > 0:
        entries = block_levels(rng, extent, cuts, -0.22, 0.18) * entries
    return jnp.clip(entries, min=-most, max=most).astype(kind)


def setup_inputs(seed: int = 0) -> dict:
    key_of = jax.random.split(jax.random.key(seed), 7)
    return {
        "activations": gaussian(key_of[0], (TOKENS, 2 * D), 1.0, 6.0, ((0, 4), (1, 8))),
        "top_lists": distinct(key_of[1], TOKENS, FEATURES, TOPK, 256),
        "encoder_weight": gaussian(key_of[2], (2 * D, FEATURES), (2 * D) ** -0.5, 0.0625, ((1, 8),)),
        "encoder_bias": gaussian(key_of[3], (FEATURES,), 0.5, 3.0, ((0, 8),), jnp.float32),
        "decoder_weight": gaussian(key_of[4], (2 * D, FEATURES), (32 * TOPK) ** -0.5, 0.125, ((1, 8),)),
        "decoder_bias": gaussian(key_of[5], (2 * D,), 0.5, 3.0, (), jnp.float32),
    }


def contract_rows(left, right):
    return lax.dot_general(left, right, (((0,), (0,)), ((), ())), preferred_element_type=jnp.float32)


def reference(activations, top_lists, encoder_weight, encoder_bias, decoder_weight, decoder_bias):
    token_count = activations.shape[0]
    encoded = jnp.dot(activations, encoder_weight, preferred_element_type=jnp.float32) + encoder_bias
    row_ids = jnp.arange(token_count, dtype=jnp.int32)[:, None]
    chosen = jnp.zeros(encoded.shape, jnp.float32).at[row_ids, top_lists].set(1.0)
    codes = jnp.where(chosen > 0.0, encoded, 0.0).astype(jnp.bfloat16)
    rebuilt = lax.dot_general(codes, decoder_weight, (((1,), (1,)), ((), ())), preferred_element_type=jnp.float32)
    error = (rebuilt + decoder_bias - activations.astype(jnp.float32)).astype(jnp.bfloat16)
    pulled = jnp.dot(error, decoder_weight, preferred_element_type=jnp.float32)
    code_grads = jnp.where(chosen > 0.0, pulled, 0.0).astype(jnp.bfloat16)
    encoder_grad = contract_rows(activations, code_grads)
    decoder_grad = contract_rows(error, codes)
    return encoder_grad, decoder_grad
```

```python
import functools

import jax
import jax.numpy as jnp
from jax import lax
from jax.experimental import pallas as pl
from jax.experimental.pallas import tpu as pltpu
from jax.sharding import PartitionSpec as P

ROWS = 128


def pick(values, lanes):
    return jnp.take_along_axis(values, lanes, axis=1, mode="promise_in_bounds")


def place_kernel(width, ids_ref, out_ref):
    rows, top = ids_ref.shape[1:]
    chunks = out_ref.shape[2] // width
    base = pl.program_id(0) * top
    lane = lax.broadcasted_iota(jnp.int32, (8, width), 1)

    def group(step, carry):
        at = pl.ds(pl.multiple_of(step * 8, 8), 8)
        ids = ids_ref[0, at, :]
        found = [jnp.full((8, width), -1, jnp.int32)] * chunks
        for k in range(top):
            relative = jnp.broadcast_to(ids[:, k : k + 1], (8, width)) - lane
            found = [jnp.where(relative == c * width, k, found[c]) for c in range(chunks)]
        for c in range(chunks):
            out_ref[0, at, c * width : (c + 1) * width] = jnp.where(
                found[c] >= 0, found[c] + base, -1
            )
        return carry

    lax.fori_loop(0, rows // 8, group, 0)


def place(ids, features, width):
    packs, rows, top = ids.shape
    return pl.pallas_call(
        functools.partial(place_kernel, width),
        grid=(packs, rows // ROWS),
        in_specs=[pl.BlockSpec((1, ROWS, top), lambda h, i: (h, i, 0))],
        out_specs=pl.BlockSpec((1, ROWS, features), lambda h, i: (h, i, 0)),
        out_shape=jax.ShapeDtypeStruct((packs, rows, features), jnp.int32),
        cost_estimate=pl.CostEstimate(
            flops=packs * rows * top * features * 20, bytes_accessed=packs * rows * features * 4,
            transcendentals=0,
        ),
        name="place",
    )(ids)


def project_kernel(width, rows_ref, weight_ref, ids_ref, bias_ref, out_ref):
    packs, rows, depth = rows_ref.shape
    chunks = weight_ref.shape[1] // width
    total = jnp.zeros((rows, width), jnp.float32)
    for h in range(packs):
        ids = ids_ref[h]
        chunk = lax.shift_right_arithmetic(ids, width.bit_length() - 1)
        lanes = lax.bitwise_and(ids, width - 1)
        for pair in range(0, chunks, 2):
            cols = slice(pair * width, (pair + 2) * width)
            product = jnp.dot(
                rows_ref[h], weight_ref[:, cols], preferred_element_type=jnp.float32
            ) + bias_ref[:, cols]
            for c in range(2):
                got = pick(product[:, c * width : (c + 1) * width], lanes)
                total = jnp.where(chunk == pair + c, got, total)
    out_ref[...] = total


def project(rows, weight, ids, bias, width):
    packs, count, depth = rows.shape
    features = weight.shape[1]
    return pl.pallas_call(
        functools.partial(project_kernel, width),
        grid=(count // ROWS,),
        in_specs=[
            pl.BlockSpec((packs, ROWS, depth), lambda i: (0, i, 0)),
            pl.BlockSpec((depth, features), lambda i: (0, 0)),
            pl.BlockSpec((packs, ROWS, width), lambda i: (0, i, 0)),
            pl.BlockSpec((1, features), lambda i: (0, 0)),
        ],
        out_specs=pl.BlockSpec((ROWS, width), lambda i: (i, 0)),
        out_shape=jax.ShapeDtypeStruct((count, width), jnp.float32),
        cost_estimate=pl.CostEstimate(
            flops=2 * packs * count * depth * features,
            bytes_accessed=rows.size * 2 + weight.size * 2, transcendentals=0,
        ),
        name="project",
    )(rows, weight, ids, bias)


def spread_kernel(width, packed_ref, place_ref, out_ref):
    packed = packed_ref[...].astype(jnp.float32)
    for h in range(place_ref.shape[0]):
        for c in range(place_ref.shape[2] // width):
            cols = slice(c * width, (c + 1) * width)
            at = place_ref[h, :, cols]
            got = pick(packed, jnp.maximum(at, 0))
            out_ref[h, :, cols] = jnp.where(at >= 0, got, 0.0).astype(jnp.bfloat16)


def spread(packed, places):
    packs, count, features = places.shape
    width = packed.shape[1]
    return pl.pallas_call(
        functools.partial(spread_kernel, width),
        grid=(count // ROWS,),
        in_specs=[
            pl.BlockSpec((ROWS, width), lambda i: (i, 0)),
            pl.BlockSpec((packs, ROWS, features), lambda i: (0, i, 0)),
        ],
        out_specs=pl.BlockSpec((packs, ROWS, features), lambda i: (0, i, 0)),
        out_shape=jax.ShapeDtypeStruct(places.shape, jnp.bfloat16),
        cost_estimate=pl.CostEstimate(
            flops=places.size * 4, bytes_accessed=places.size * 6, transcendentals=0
        ),
        name="spread",
    )(packed, places)


def contract_rows(left, right):
    return lax.dot_general(
        left, right, (((0,), (0,)), ((), ())), preferred_element_type=jnp.float32
    )


MESH = pl.DeviceIdType.MESH


def for_each(count, step):
    lax.fori_loop(0, count, lambda i, carry: (step(i), carry)[1], 0)


def meet(shards, groups, owner, group):
    barrier = pltpu.get_barrier_semaphore()

    def greet_owner(step):
        peer = lax.rem(owner + 1 + step, shards)
        pl.semaphore_signal(barrier, inc=1, device_id={"feat": peer}, device_id_type=MESH)

    def greet_group(step):
        peer = lax.rem(group + 1 + step, groups)
        pl.semaphore_signal(barrier, inc=1, device_id={"tok": peer}, device_id_type=MESH)

    for_each(shards - 1, greet_owner)
    for_each(groups - 1, greet_group)
    pl.semaphore_wait(barrier, shards + groups - 2)


def tail_kernel(
    shards, groups, error_hbm, inputs_hbm, codes_hbm, weight_hbm, ids_hbm, places_hbm,
    decoder_out, encoder_out,
    error, inputs, codes, weight, ids, places, part, part_in, share, share_in,
    decoder_send, decoder_in, encoder_send, encoder_in,
    load_sem, codes_sem, places_sem, part_send, part_recv, share_send, share_recv,
    block_send, block_recv, home_send, home_recv,
):
    owner, group = lax.axis_index("feat"), lax.axis_index("tok")
    packs, packed_rows, hidden_dev = error.shape
    width = ids.shape[2]
    features = weight.shape[1]
    tile = packed_rows // shards
    per = shards // groups
    pairs = shards // 2
    all_rows = packs * packed_rows

    loads = [
        pltpu.make_async_copy(source, target, load_sem.at[k])
        for k, (source, target) in enumerate(
            ((error_hbm, error), (weight_hbm, weight), (ids_hbm, ids), (inputs_hbm, inputs))
        )
    ]

    def pair_cols(pair):
        return pl.ds(pl.multiple_of(pair * 2 * width, 2 * width), 2 * width)

    def codes_load(pair):
        cols = pair_cols(pair)
        return pltpu.make_async_copy(
            codes_hbm.at[:, :, cols], codes.at[:, :, cols], codes_sem.at[pair]
        )

    def rows_of(step):
        return pl.ds(pl.multiple_of(step * tile, tile), tile)

    def places_load(step, slot):
        return pltpu.make_async_copy(
            places_hbm.at[:, rows_of(step), :], places.at[slot], places_sem.at[slot]
        )

    for load in loads[:3]:
        load.start()
    for_each(pairs, lambda pair: codes_load(pair).start())
    loads[3].start()
    places_load(0, 0).start()
    meet(shards, groups, owner, group)
    for load in loads[:3]:
        load.wait()

    def part_copy(peer, slot):
        return pltpu.make_async_remote_copy(
            src_ref=part.at[peer], dst_ref=part_in.at[slot], send_sem=part_send.at[peer],
            recv_sem=part_recv.at[slot], device_id={"feat": peer}, device_id_type=MESH,
        )

    def project_tile(step):
        peer = lax.rem(owner + 1 + step, shards)
        at = rows_of(peer)
        rows = error[:, at, :].reshape(packs * tile, hidden_dev)
        here = [ids[h, at, :] for h in range(packs)]
        chunk = [lax.shift_right_arithmetic(i, width.bit_length() - 1) for i in here]
        lanes = [lax.bitwise_and(i, width - 1) for i in here]

        def add_pair(pair, total):
            product = jnp.dot(
                rows, weight[:, pair_cols(pair)], preferred_element_type=jnp.float32
            )
            for h in range(packs):
                for c in range(2):
                    got = pick(
                        product[h * tile : (h + 1) * tile, c * width : (c + 1) * width], lanes[h]
                    )
                    total = jnp.where(chunk[h] == 2 * pair + c, got, total)
            return total

        total = jnp.zeros((tile, width), jnp.float32)
        if pairs <= 4:
            for pair in range(pairs):
                total = add_pair(pair, total)
        else:
            total = lax.fori_loop(0, pairs, add_pair, total)
        part[peer] = total

        @pl.when(step < shards - 1)
        def _():
            part_copy(peer, owner).start()

    for_each(shards, project_tile)

    def gradient(left, pair, send):
        cols = pair_cols(pair)
        block = contract_rows(
            left[...].reshape(all_rows, hidden_dev),
            codes[:, :, cols].reshape(all_rows, 2 * width),
        ).astype(jnp.bfloat16)
        send[2 * pair] = block[:, :width]
        send[2 * pair + 1] = block[:, width:]

    def decoder_pair(pair):
        codes_load(pair).wait()
        gradient(error, pair, decoder_send)

    for_each(pairs, decoder_pair)

    def add_part(step, total):
        peer = lax.rem(owner + shards - 1 - step, shards)
        part_copy(peer, peer).wait_recv()
        return total + part_in[peer]

    total = lax.fori_loop(0, shards - 1, add_part, part[owner])
    share[...] = total.astype(jnp.bfloat16)
    share_in[owner] = share[...]

    def share_copy(peer, slot):
        return pltpu.make_async_remote_copy(
            src_ref=share, dst_ref=share_in.at[slot], send_sem=share_send.at[peer],
            recv_sem=share_recv.at[slot], device_id={"feat": peer}, device_id_type=MESH,
        )

    def block_copy(k, send, came, peer, slot):
        return pltpu.make_async_remote_copy(
            src_ref=send.at[peer], dst_ref=came.at[slot], send_sem=block_send.at[k, peer],
            recv_sem=block_recv.at[k, slot], device_id={"feat": peer}, device_id_type=MESH,
        )

    def others(step):
        return lax.rem(owner + 1 + step, shards)

    for_each(shards - 1, lambda step: share_copy(others(step), owner).start())
    for_each(
        shards - 1,
        lambda step: block_copy(0, decoder_send, decoder_in, others(step), owner).start(),
    )
    for_each(
        shards - 1, lambda step: share_copy(others(step), others(step)).wait_recv()
    )
    loads[3].wait()

    def spread_tile(step):
        slot = lax.rem(step, 2)

        @pl.when(step + 1 < shards)
        def _():
            places_load(step + 1, 1 - slot).start()

        places_load(step, slot).wait()
        packed = share_in[step].astype(jnp.float32)
        for h in range(packs):
            for c in range(features // width):
                cols = slice(c * width, (c + 1) * width)
                at = places[slot, h, :, cols]
                got = pick(packed, jnp.maximum(at, 0))
                codes[h, rows_of(step), cols] = jnp.where(at >= 0, got, 0.0).astype(jnp.bfloat16)

    for_each(shards, spread_tile)

    def encoder_pair(step):
        pair = lax.rem(owner // 2 + 1 + step, pairs)
        gradient(inputs, pair, encoder_send)
        for k in range(2):
            peer = 2 * pair + k

            @pl.when(peer != owner)
            def _():
                block_copy(1, encoder_send, encoder_in, peer, owner).start()

    for_each(pairs, encoder_pair)

    def home_slice(out, source, group_from):
        at = pl.ds(pl.multiple_of(lax.rem(source, per) * hidden_dev, hidden_dev), hidden_dev)
        return out.at[at, pl.ds(pl.multiple_of(group_from * width, width), width)]

    def home_remote(k, block, out, source):
        target = source // per
        return pltpu.make_async_remote_copy(
            src_ref=block, dst_ref=home_slice(out, source, group),
            send_sem=home_send.at[k, source],
            recv_sem=home_recv.at[k, group * per + lax.rem(source, per)],
            device_id={"tok": target}, device_id_type=MESH,
        )

    def home_local(k, block, out, source):
        return pltpu.make_async_copy(
            block, home_slice(out, source, group),
            home_recv.at[k, group * per + lax.rem(source, per)],
        )

    def go_home(k, block, out, source):
        stays = source // per == group

        @pl.when(stays)
        def _():
            home_local(k, block, out, source).start()

        @pl.when(jnp.logical_not(stays))
        def _():
            home_remote(k, block, out, source).start()

    def relay(k, send, came, out):
        go_home(k, send.at[owner], out, owner)

        def forward(step):
            source = lax.rem(owner + shards - 1 - step, shards)
            block_copy(k, send, came, source, source).wait_recv()
            go_home(k, came.at[source], out, source)

        for_each(shards - 1, forward)

    relay(0, decoder_send, decoder_in, decoder_out)
    relay(1, encoder_send, encoder_in, encoder_out)

    def finish(k, send, came, out):
        def arrive(index):
            source = index // per

            @pl.when(source == group)
            def _():
                home_local(k, send.at[0], out, group * per + lax.rem(index, per)).wait()

            @pl.when(source != group)
            def _():
                pltpu.make_async_remote_copy(
                    src_ref=send.at[0],
                    dst_ref=home_slice(out, lax.rem(index, per), source),
                    send_sem=home_send.at[k, 0], recv_sem=home_recv.at[k, index],
                    device_id={"tok": source}, device_id_type=MESH,
                ).wait_recv()

        for_each(groups * per, arrive)

        def sent(step):
            peer = others(step)
            block_copy(k, send, came, peer, owner).wait_send()

        for_each(shards - 1, sent)

        def relayed(source):
            @pl.when(source // per != group)
            def _():
                home_remote(k, send.at[0], out, source).wait_send()

        for_each(shards, relayed)

    finish(0, decoder_send, decoder_in, decoder_out)
    finish(1, encoder_send, encoder_in, encoder_out)
    for_each(shards - 1, lambda step: part_copy(others(step), owner).wait_send())
    for_each(shards - 1, lambda step: share_copy(others(step), owner).wait_send())


def tail(shards, groups, error, inputs, codes, weight, ids, places):
    packs, packed_rows, width = ids.shape
    hidden_dev = weight.shape[0]
    features = weight.shape[1]
    tile = packed_rows // shards
    per = shards // groups
    flat = (packs, packed_rows, hidden_dev)
    bf16, f32 = jnp.bfloat16, jnp.float32
    dma = pltpu.SemaphoreType.DMA
    home = jax.ShapeDtypeStruct((per * hidden_dev, groups * width), bf16)
    anywhere = pl.BlockSpec(memory_space=pl.ANY)
    return pl.pallas_call(
        functools.partial(tail_kernel, shards, groups),
        in_specs=[anywhere] * 6,
        out_specs=[anywhere] * 2,
        out_shape=[home, home],
        scratch_shapes=[
            pltpu.VMEM(flat, bf16),
            pltpu.VMEM(flat, bf16),
            pltpu.VMEM((packs, packed_rows, features), bf16),
            pltpu.VMEM(weight.shape, bf16),
            pltpu.VMEM(ids.shape, jnp.int32),
            pltpu.VMEM((2, packs, tile, features), jnp.int32),
            pltpu.VMEM((shards, tile, width), f32),
            pltpu.VMEM((shards, tile, width), f32),
            pltpu.VMEM((tile, width), bf16),
            pltpu.VMEM((shards, tile, width), bf16),
            *[pltpu.VMEM((shards, hidden_dev, width), bf16)] * 4,
            dma((4,)), dma((shards // 2,)), dma((2,)),
            dma((shards,)), dma((shards,)), dma((shards,)), dma((shards,)),
            dma((2, shards)), dma((2, shards)), dma((2, shards)), dma((2, groups * per)),
        ],
        compiler_params=pltpu.CompilerParams(
            collective_id=0, has_side_effects=True, vmem_limit_bytes=60 * 1024 * 1024
        ),
        name="tail",
    )(error.reshape(flat), inputs.reshape(flat), codes.reshape(packs, packed_rows, features),
      weight, ids, places)


def body(activations, top_lists, encoder_weight, encoder_bias, decoder_weight, decoder_bias):
    group_rows, hidden_dev = activations.shape
    feat_dev = encoder_weight.shape[1]
    top = top_lists.shape[1]
    shards, groups = lax.axis_size("feat"), lax.axis_size("tok")
    owner, group = lax.axis_index("feat"), lax.axis_index("tok")
    width = feat_dev // groups
    features = shards * width
    packs = width // top
    all_rows = group_rows * groups

    def own_columns(weight):
        return lax.dynamic_slice_in_dim(weight, group * width, width, 1)

    lists = lax.all_gather(top_lists, "tok", axis=0, tiled=True)
    inputs = lax.all_gather(activations, "tok", axis=0, tiled=True)
    both = jnp.concatenate([own_columns(encoder_weight), own_columns(decoder_weight)], axis=1)
    arrived = lax.all_to_all(
        both.reshape(shards, hidden_dev, 2 * width), "feat", split_axis=0, concat_axis=0, tiled=True
    )

    in_block = lists % feat_dev
    local = jnp.where(
        in_block // width == group, lists // feat_dev * width + in_block % width, -1
    ).reshape(packs, all_rows // packs, top)
    packed_ids = jnp.stack(
        [
            jnp.pad(local[h], ((0, 0), (h * top, width - (h + 1) * top)), constant_values=-1)
            for h in range(packs)
        ]
    )
    places = place(local, features, width)
    arrived, places = lax.optimization_barrier((arrived, places))
    encoder_own, decoder_own = (
        arrived[:, :, at : at + width].transpose(1, 0, 2).reshape(hidden_dev, features)
        for at in (0, width)
    )
    bias = lax.dynamic_update_slice(
        jnp.zeros((1, features), jnp.float32),
        lax.dynamic_slice_in_dim(encoder_bias, group * width, width)[None, :],
        (0, owner * width),
    )

    def packed_sum(rows, weight, offset):
        part = project(rows.reshape(packs, all_rows // packs, hidden_dev), weight, packed_ids, offset, width)
        terms = lax.all_to_all(
            part.reshape(shards, -1, width), "feat", split_axis=0, concat_axis=0, tiled=True
        )
        share = jnp.sum(terms, axis=0).astype(jnp.bfloat16)
        copies = jnp.broadcast_to(share, (shards, *share.shape))
        return lax.all_to_all(copies, "feat", split_axis=0, concat_axis=0, tiled=True).reshape(-1, width)

    def spread_rows(packed):
        return spread(packed, places).reshape(all_rows, features)

    codes = spread_rows(packed_sum(inputs, encoder_own, bias))
    rebuilt = lax.psum_scatter(
        lax.dot_general(
            codes, decoder_own, (((1,), (1,)), ((), ())), preferred_element_type=jnp.float32
        ).astype(jnp.bfloat16),
        "tok",
        scatter_dimension=0,
        tiled=True,
    )
    own_bias = lax.dynamic_slice_in_dim(decoder_bias, owner * hidden_dev, hidden_dev)
    error_rows = (
        rebuilt.astype(jnp.float32) + own_bias - activations.astype(jnp.float32)
    ).astype(jnp.bfloat16)
    error = lax.all_gather(error_rows, "tok", axis=0, tiled=True)

    decoder_grad, encoder_grad = tail(
        shards, groups, error, inputs, codes, decoder_own, packed_ids, places
    )
    return encoder_grad.astype(jnp.float32), decoder_grad.astype(jnp.float32)


def solution(mesh):
    return jax.shard_map(
        body,
        mesh=mesh,
        in_specs=(
            P("tok", "feat"),
            P("tok", None),
            P(None, "feat"),
            P("feat"),
            P(None, "feat"),
            P(),
        ),
        out_specs=(P("tok", "feat"), P("tok", "feat")),
        check_vma=False,
    )
```

```python
import functools

import jax
import jax.numpy as jnp
from jax import lax
from jax.experimental import pallas as pl
from jax.experimental.pallas import tpu as pltpu
from jax.sharding import PartitionSpec as P

def pick(values, lanes):
    return jnp.take_along_axis(values, lanes, axis=1, mode="promise_in_bounds")


def contract_rows(left, right):
    return lax.dot_general(
        left, right, (((0,), (0,)), ((), ())), preferred_element_type=jnp.float32
    )


MESH = pl.DeviceIdType.MESH


def for_each(count, step):
    lax.fori_loop(0, count, lambda i, carry: (step(i), carry)[1], 0)


def meet(shards, groups, owner, group):
    barrier = pltpu.get_barrier_semaphore()

    def greet_owner(step):
        peer = lax.rem(owner + 1 + step, shards)
        pl.semaphore_signal(barrier, inc=1, device_id={"feat": peer}, device_id_type=MESH)

    def greet_group(step):
        peer = lax.rem(group + 1 + step, groups)
        pl.semaphore_signal(barrier, inc=1, device_id={"tok": peer}, device_id_type=MESH)

    for_each(shards - 1, greet_owner)
    for_each(groups - 1, greet_group)
    pl.semaphore_wait(barrier, shards + groups - 2)


def tail_kernel(
    shards, groups, error_hbm, inputs_hbm, codes_hbm, weight_hbm, ids_hbm, places_hbm,
    decoder_out, encoder_out,
    error, inputs, codes, weight, ids, places, part, part_in, share, share_in,
    decoder_send, decoder_in, encoder_send, encoder_in,
    load_sem, codes_sem, places_sem, part_send, part_recv, share_send, share_recv,
    block_send, block_recv, home_send, home_recv,
):
    owner, group = lax.axis_index("feat"), lax.axis_index("tok")
    packs, packed_rows, hidden_dev = error.shape
    width = ids.shape[2]
    features = weight.shape[1]
    tile = packed_rows // shards
    per = shards // groups
    pairs = shards // 2
    all_rows = packs * packed_rows

    loads = [
        pltpu.make_async_copy(source, target, load_sem.at[k])
        for k, (source, target) in enumerate(
            ((error_hbm, error), (weight_hbm, weight), (ids_hbm, ids), (inputs_hbm, inputs))
        )
    ]

    def pair_cols(pair):
        return pl.ds(pl.multiple_of(pair * 2 * width, 2 * width), 2 * width)

    def codes_load(pair):
        cols = pair_cols(pair)
        return pltpu.make_async_copy(
            codes_hbm.at[:, :, cols], codes.at[:, :, cols], codes_sem.at[pair]
        )

    def rows_of(step):
        return pl.ds(pl.multiple_of(step * tile, tile), tile)

    def places_load(step, slot):
        return pltpu.make_async_copy(
            places_hbm.at[:, rows_of(step), :], places.at[slot], places_sem.at[slot]
        )

    for load in loads[:3]:
        load.start()
    for_each(pairs, lambda pair: codes_load(pair).start())
    loads[3].start()
    places_load(0, 0).start()
    meet(shards, groups, owner, group)
    for load in loads[:3]:
        load.wait()

    def part_copy(peer, slot):
        return pltpu.make_async_remote_copy(
            src_ref=part.at[peer], dst_ref=part_in.at[slot], send_sem=part_send.at[peer],
            recv_sem=part_recv.at[slot], device_id={"feat": peer}, device_id_type=MESH,
        )

    def project_tile(step):
        peer = lax.rem(owner + 1 + step, shards)
        at = rows_of(peer)
        rows = error[:, at, :].reshape(packs * tile, hidden_dev)
        here = [ids[h, at, :] for h in range(packs)]
        chunk = [lax.shift_right_arithmetic(i, width.bit_length() - 1) for i in here]
        lanes = [lax.bitwise_and(i, width - 1) for i in here]

        def add_pair(pair, total):
            product = jnp.dot(
                rows, weight[:, pair_cols(pair)], preferred_element_type=jnp.float32
            )
            for h in range(packs):
                for c in range(2):
                    got = pick(
                        product[h * tile : (h + 1) * tile, c * width : (c + 1) * width], lanes[h]
                    )
                    total = jnp.where(chunk[h] == 2 * pair + c, got, total)
            return total

        total = jnp.zeros((tile, width), jnp.float32)
        if pairs <= 4:
            for pair in range(pairs):
                total = add_pair(pair, total)
        else:
            total = lax.fori_loop(0, pairs, add_pair, total)
        part[peer] = total

        @pl.when(step < shards - 1)
        def _():
            part_copy(peer, owner).start()

    for_each(shards, project_tile)

    def gradient(left, pair, send):
        cols = pair_cols(pair)
        block = contract_rows(
            left[...].reshape(all_rows, hidden_dev),
            codes[:, :, cols].reshape(all_rows, 2 * width),
        ).astype(jnp.bfloat16)
        send[2 * pair] = block[:, :width]
        send[2 * pair + 1] = block[:, width:]

    def decoder_pair(pair):
        codes_load(pair).wait()
        gradient(error, pair, decoder_send)

    for_each(pairs, decoder_pair)

    def add_part(step, total):
        peer = lax.rem(owner + shards - 1 - step, shards)
        part_copy(peer, peer).wait_recv()
        return total + part_in[peer]

    total = lax.fori_loop(0, shards - 1, add_part, part[owner])
    share[...] = total.astype(jnp.bfloat16)
    share_in[owner] = share[...]

    def share_copy(peer, slot):
        return pltpu.make_async_remote_copy(
            src_ref=share, dst_ref=share_in.at[slot], send_sem=share_send.at[peer],
            recv_sem=share_recv.at[slot], device_id={"feat": peer}, device_id_type=MESH,
        )

    def block_copy(k, send, came, peer, slot):
        return pltpu.make_async_remote_copy(
            src_ref=send.at[peer], dst_ref=came.at[slot], send_sem=block_send.at[k, peer],
            recv_sem=block_recv.at[k, slot], device_id={"feat": peer}, device_id_type=MESH,
        )

    def others(step):
        return lax.rem(owner + 1 + step, shards)

    for_each(shards - 1, lambda step: share_copy(others(step), owner).start())
    for_each(
        shards - 1,
        lambda step: block_copy(0, decoder_send, decoder_in, others(step), owner).start(),
    )
    for_each(
        shards - 1, lambda step: share_copy(others(step), others(step)).wait_recv()
    )
    loads[3].wait()

    def spread_tile(step):
        slot = lax.rem(step, 2)

        @pl.when(step + 1 < shards)
        def _():
            places_load(step + 1, 1 - slot).start()

        places_load(step, slot).wait()
        packed = share_in[step].astype(jnp.float32)
        for h in range(packs):
            for c in range(features // width):
                cols = slice(c * width, (c + 1) * width)
                at = places[slot, h, :, cols]
                got = pick(packed, jnp.maximum(at, 0))
                codes[h, rows_of(step), cols] = jnp.where(at >= 0, got, 0.0).astype(jnp.bfloat16)

    for_each(shards, spread_tile)

    def encoder_pair(step):
        pair = lax.rem(owner // 2 + 1 + step, pairs)
        gradient(inputs, pair, encoder_send)
        for k in range(2):
            peer = 2 * pair + k

            @pl.when(peer != owner)
            def _():
                block_copy(1, encoder_send, encoder_in, peer, owner).start()

    for_each(pairs, encoder_pair)

    def home_slice(out, source, group_from):
        at = pl.ds(pl.multiple_of(lax.rem(source, per) * hidden_dev, hidden_dev), hidden_dev)
        return out.at[at, pl.ds(pl.multiple_of(group_from * width, width), width)]

    def home_remote(k, block, out, source):
        target = source // per
        return pltpu.make_async_remote_copy(
            src_ref=block, dst_ref=home_slice(out, source, group),
            send_sem=home_send.at[k, source],
            recv_sem=home_recv.at[k, group * per + lax.rem(source, per)],
            device_id={"tok": target}, device_id_type=MESH,
        )

    def home_local(k, block, out, source):
        return pltpu.make_async_copy(
            block, home_slice(out, source, group),
            home_recv.at[k, group * per + lax.rem(source, per)],
        )

    def go_home(k, block, out, source):
        stays = source // per == group

        @pl.when(stays)
        def _():
            home_local(k, block, out, source).start()

        @pl.when(jnp.logical_not(stays))
        def _():
            home_remote(k, block, out, source).start()

    def relay(k, send, came, out):
        go_home(k, send.at[owner], out, owner)

        def forward(step):
            source = lax.rem(owner + shards - 1 - step, shards)
            block_copy(k, send, came, source, source).wait_recv()
            go_home(k, came.at[source], out, source)

        for_each(shards - 1, forward)

    relay(0, decoder_send, decoder_in, decoder_out)
    relay(1, encoder_send, encoder_in, encoder_out)

    def finish(k, send, came, out):
        def arrive(index):
            source = index // per

            @pl.when(source == group)
            def _():
                home_local(k, send.at[0], out, group * per + lax.rem(index, per)).wait()

            @pl.when(source != group)
            def _():
                pltpu.make_async_remote_copy(
                    src_ref=send.at[0],
                    dst_ref=home_slice(out, lax.rem(index, per), source),
                    send_sem=home_send.at[k, 0], recv_sem=home_recv.at[k, index],
                    device_id={"tok": source}, device_id_type=MESH,
                ).wait_recv()

        for_each(groups * per, arrive)

        def sent(step):
            peer = others(step)
            block_copy(k, send, came, peer, owner).wait_send()

        for_each(shards - 1, sent)

        def relayed(source):
            @pl.when(source // per != group)
            def _():
                home_remote(k, send.at[0], out, source).wait_send()

        for_each(shards, relayed)

    finish(0, decoder_send, decoder_in, decoder_out)
    finish(1, encoder_send, encoder_in, encoder_out)
    for_each(shards - 1, lambda step: part_copy(others(step), owner).wait_send())
    for_each(shards - 1, lambda step: share_copy(others(step), owner).wait_send())


def tail(shards, groups, error, inputs, codes, weight, ids, places):
    packs, packed_rows, width = ids.shape
    hidden_dev = weight.shape[0]
    features = weight.shape[1]
    tile = packed_rows // shards
    per = shards // groups
    flat = (packs, packed_rows, hidden_dev)
    bf16, f32 = jnp.bfloat16, jnp.float32
    dma = pltpu.SemaphoreType.DMA
    home = jax.ShapeDtypeStruct((per * hidden_dev, groups * width), bf16)
    anywhere = pl.BlockSpec(memory_space=pl.ANY)
    return pl.pallas_call(
        functools.partial(tail_kernel, shards, groups),
        in_specs=[anywhere] * 6,
        out_specs=[anywhere] * 2,
        out_shape=[home, home],
        scratch_shapes=[
            pltpu.VMEM(flat, bf16),
            pltpu.VMEM(flat, bf16),
            pltpu.VMEM((packs, packed_rows, features), bf16),
            pltpu.VMEM(weight.shape, bf16),
            pltpu.VMEM(ids.shape, jnp.int32),
            pltpu.VMEM((2, packs, tile, features), jnp.int32),
            pltpu.VMEM((shards, tile, width), f32),
            pltpu.VMEM((shards, tile, width), f32),
            pltpu.VMEM((tile, width), bf16),
            pltpu.VMEM((shards, tile, width), bf16),
            *[pltpu.VMEM((shards, hidden_dev, width), bf16)] * 4,
            dma((4,)), dma((shards // 2,)), dma((2,)),
            dma((shards,)), dma((shards,)), dma((shards,)), dma((shards,)),
            dma((2, shards)), dma((2, shards)), dma((2, shards)), dma((2, groups * per)),
        ],
        compiler_params=pltpu.CompilerParams(
            collective_id=0, has_side_effects=True, vmem_limit_bytes=60 * 1024 * 1024
        ),
        name="tail",
    )(error.reshape(flat), inputs.reshape(flat), codes.reshape(packs, packed_rows, features),
      weight, ids, places)


def front_kernel(
    shards, groups, packs, top,
    acts_hbm, lists_hbm, encoder_hbm, decoder_hbm, bias_hbm,
    codes_out, ids_out, places_out, decoder_out, inputs_out,
    inputs, lists, ids, weight, bias, own_block, places, codes,
    part, part_in, share, share_in,
    load_sem, store_sem, gather_send, gather_recv, encoder_send, encoder_recv, decoder_send,
    decoder_recv, places_sem, codes_sem, part_send, part_recv, share_send, share_recv,
):
    owner, group = lax.axis_index("feat"), lax.axis_index("tok")
    all_rows, hidden_dev = inputs.shape
    width = ids.shape[1]
    features = weight.shape[1]
    feat_dev = encoder_hbm.shape[1]
    group_rows = all_rows // groups
    packed_rows = all_rows // packs
    tile = packed_rows // shards
    pairs = shards // 2
    far = lax.rem(group + groups // 2, groups)
    near = group + 1 - 2 * lax.rem(group, 2)

    def others(step):
        return lax.rem(owner + 1 + step, shards)

    def block_rows(source):
        return pl.ds(pl.multiple_of(source * group_rows, group_rows), group_rows)

    def wide(index):
        return pl.ds(pl.multiple_of(index * width, width), width)

    def tall(index):
        return pl.ds(pl.multiple_of(index * hidden_dev, hidden_dev), hidden_dev)

    def rows_of(step):
        return pl.ds(pl.multiple_of(step * tile, tile), tile)

    def pack_rows(h, step):
        return pl.ds(pl.multiple_of(h * packed_rows + step * tile, tile), tile)

    def gather_copy(k, hop, rows_from, peer):
        own, held = ((lists_hbm, lists), (acts_hbm, inputs))[k]
        source = own if hop < 2 else held.at[block_rows(rows_from)]
        return pltpu.make_async_remote_copy(
            src_ref=source, dst_ref=held.at[block_rows(rows_from)],
            send_sem=gather_send.at[k, hop], recv_sem=gather_recv.at[k, hop],
            device_id={"tok": peer}, device_id_type=MESH,
        )

    def encoder_copy(peer, slot):
        return pltpu.make_async_remote_copy(
            src_ref=encoder_hbm.at[tall(peer), wide(group)], dst_ref=weight.at[:, wide(slot)],
            send_sem=encoder_send.at[peer], recv_sem=encoder_recv.at[slot],
            device_id={"feat": peer}, device_id_type=MESH,
        )

    def decoder_copy(peer, slot):
        return pltpu.make_async_remote_copy(
            src_ref=decoder_hbm.at[tall(peer), wide(group)], dst_ref=decoder_out.at[:, wide(slot)],
            send_sem=decoder_send.at[peer], recv_sem=decoder_recv.at[slot],
            device_id={"feat": peer}, device_id_type=MESH,
        )

    loads = [
        pltpu.make_async_copy(source, target, load_sem.at[k])
        for k, (source, target) in enumerate(
            (
                (lists_hbm, lists.at[block_rows(group)]),
                (acts_hbm, inputs.at[block_rows(group)]),
                (encoder_hbm.at[tall(owner), wide(group)], weight.at[:, wide(owner)]),
                (bias_hbm, bias),
                (decoder_hbm.at[tall(owner), wide(group)], own_block),
            )
        )
    ]
    for load in loads:
        load.start()
    meet(shards, groups, owner, group)
    for k in range(2):
        gather_copy(k, 0, group, far).start()
        gather_copy(k, 1, group, near).start()
    for_each(shards - 1, lambda step: encoder_copy(others(step), owner).start())
    early = shards // 2
    for_each(early, lambda step: decoder_copy(others(step), owner).start())

    def gather(k):
        loads[k].wait()
        gather_copy(k, 0, far, far).wait_recv()
        gather_copy(k, 2, far, near).start()
        gather_copy(k, 1, near, near).wait_recv()

    def gather_last(k):
        gather_copy(k, 2, lax.rem(near + groups // 2, groups), near).wait_recv()

    gather(0)
    gather_last(0)

    def own_ids(step):
        at = pl.ds(pl.multiple_of(step * tile, tile), tile)
        raw = lists[at, :]
        within = lax.bitwise_and(raw, feat_dev - 1)
        local = lax.shift_right_arithmetic(raw, feat_dev.bit_length() - 1) * width + lax.bitwise_and(
            raw, width - 1
        )
        mine = lax.shift_right_arithmetic(within, width.bit_length() - 1) == group
        ids[at, :] = jnp.where(mine & (raw >= 0), local, -1)

    for_each(packs * shards, own_ids)
    ids_store = pltpu.make_async_copy(ids, ids_out, store_sem.at[0])
    ids_store.start()
    gather(1)

    lane = lax.broadcasted_iota(jnp.int32, (8, width), 1)
    chunks = features // width

    def places_copy(step, slot):
        return pltpu.make_async_copy(
            places.at[slot], places_out.at[:, rows_of(step), :], places_sem.at[slot]
        )

    def place_tile(step):
        slot = lax.rem(step, 2)

        @pl.when(step >= 2)
        def _():
            places_copy(step - 2, slot).wait()

        for h in range(packs):

            def rows8(sub, carry):
                at = pl.ds(pl.multiple_of(h * packed_rows + step * tile + sub * 8, 8), 8)
                here = ids[at, :]
                found = [jnp.full((8, width), -1, jnp.int32)] * chunks
                for k in range(h * top, (h + 1) * top):
                    relative = jnp.broadcast_to(here[:, k : k + 1], (8, width)) - lane
                    found = [jnp.where(relative == c * width, k, found[c]) for c in range(chunks)]
                to = pl.ds(pl.multiple_of(sub * 8, 8), 8)
                for c in range(chunks):
                    places[slot, h, to, c * width : (c + 1) * width] = found[c]
                return carry

            lax.fori_loop(0, tile // 8, rows8, 0)
        places_copy(step, slot).start()

    first, second = shards * 5 // 8, shards * 7 // 8
    for_each(first, place_tile)

    gather_last(1)
    inputs_store = pltpu.make_async_copy(inputs, inputs_out, store_sem.at[1])
    inputs_store.start()
    loads[4].wait()
    own_store = pltpu.make_async_copy(own_block, decoder_out.at[:, wide(owner)], store_sem.at[2])
    own_store.start()
    loads[2].wait()
    loads[3].wait()
    for_each(shards - 1, lambda step: encoder_copy(others(step), others(step)).wait_recv())

    def part_copy(peer, slot):
        return pltpu.make_async_remote_copy(
            src_ref=part.at[peer], dst_ref=part_in.at[slot], send_sem=part_send.at[peer],
            recv_sem=part_recv.at[slot], device_id={"feat": peer}, device_id_type=MESH,
        )

    def share_copy(peer, slot):
        return pltpu.make_async_remote_copy(
            src_ref=share, dst_ref=share_in.at[slot], send_sem=share_send.at[peer],
            recv_sem=share_recv.at[slot], device_id={"feat": peer}, device_id_type=MESH,
        )

    def project_tile(step):
        peer = lax.rem(owner + 1 + step, shards)
        rows = jnp.concatenate([inputs[pack_rows(h, peer), :] for h in range(packs)], axis=0)
        here = [ids[pack_rows(h, peer), :] for h in range(packs)]
        chunk = [lax.shift_right_arithmetic(i, width.bit_length() - 1) for i in here]
        lanes = [lax.bitwise_and(i, width - 1) for i in here]

        def add_pair(pair, total):
            cols = pl.ds(pl.multiple_of(pair * 2 * width, 2 * width), 2 * width)
            product = jnp.dot(
                rows, weight[:, cols], preferred_element_type=jnp.float32
            ) + bias[:, cols]
            for h in range(packs):
                for c in range(2):
                    got = pick(
                        product[h * tile : (h + 1) * tile, c * width : (c + 1) * width], lanes[h]
                    )
                    total = jnp.where(chunk[h] == 2 * pair + c, got, total)
            return total

        total = jnp.zeros((tile, width), jnp.float32)
        if pairs <= 4:
            for pair in range(pairs):
                total = add_pair(pair, total)
        else:
            total = lax.fori_loop(0, pairs, add_pair, total)
        part[peer] = total

        @pl.when(step < shards - 1)
        def _():
            part_copy(peer, owner).start()

    for_each(shards, project_tile)
    for_each(second - first, lambda step: place_tile(first + step))

    def add_part(step, total):
        peer = lax.rem(owner + shards - 1 - step, shards)
        part_copy(peer, peer).wait_recv()
        return total + part_in[peer]

    total = lax.fori_loop(0, shards - 1, add_part, part[owner])
    share[...] = total.astype(jnp.bfloat16)
    share_in[owner] = share[...]
    for_each(shards - 1, lambda step: share_copy(others(step), owner).start())
    for_each(
        shards - 1 - early, lambda step: decoder_copy(others(early + step), owner).start()
    )
    for_each(shards - second, lambda step: place_tile(second + step))
    for_each(2, lambda step: places_copy(shards - 2 + step, lax.rem(shards + step, 2)).wait())

    def places_load(step, slot):
        return pltpu.make_async_copy(
            places_out.at[:, rows_of(step), :], places.at[slot], places_sem.at[slot]
        )

    def codes_copy(step, slot):
        return pltpu.make_async_copy(
            codes.at[slot], codes_out.at[:, rows_of(step), :], codes_sem.at[slot]
        )

    places_load(0, 0).start()
    for_each(shards - 1, lambda step: share_copy(others(step), others(step)).wait_recv())

    def spread_tile(step):
        slot = lax.rem(step, 2)

        @pl.when(step + 1 < shards)
        def _():
            places_load(step + 1, 1 - slot).start()

        places_load(step, slot).wait()

        @pl.when(step >= 2)
        def _():
            codes_copy(step - 2, slot).wait()

        packed = share_in[step].astype(jnp.float32)
        for h in range(packs):
            for c in range(chunks):
                cols = slice(c * width, (c + 1) * width)
                at = places[slot, h, :, cols]
                got = pick(packed, jnp.maximum(at, 0))
                codes[slot, h, :, cols] = jnp.where(at >= 0, got, 0.0).astype(jnp.bfloat16)
        codes_copy(step, slot).start()

    for_each(shards, spread_tile)
    for_each(2, lambda step: codes_copy(shards - 2 + step, lax.rem(shards + step, 2)).wait())
    for_each(shards - 1, lambda step: decoder_copy(others(step), others(step)).wait_recv())
    for_each(shards - 1, lambda step: encoder_copy(others(step), owner).wait_send())
    for_each(shards - 1, lambda step: decoder_copy(others(step), owner).wait_send())
    for_each(shards - 1, lambda step: part_copy(others(step), owner).wait_send())
    for_each(shards - 1, lambda step: share_copy(others(step), owner).wait_send())
    for k in range(2):
        gather_copy(k, 0, group, far).wait_send()
        gather_copy(k, 1, group, near).wait_send()
        gather_copy(k, 2, far, near).wait_send()
    ids_store.wait()
    inputs_store.wait()
    own_store.wait()


def front(shards, groups, packs, top, activations, lists, encoder_weight, decoder_weight, bias):
    group_rows, hidden_dev = activations.shape
    width = lists.shape[1]
    features = shards * width
    all_rows = group_rows * groups
    packed_rows = all_rows // packs
    tile = packed_rows // shards
    bf16, f32, i32 = jnp.bfloat16, jnp.float32, jnp.int32
    dma = pltpu.SemaphoreType.DMA
    anywhere = pl.BlockSpec(memory_space=pl.ANY)
    return pl.pallas_call(
        functools.partial(front_kernel, shards, groups, packs, top),
        in_specs=[anywhere] * 5,
        out_specs=[anywhere] * 5,
        out_shape=[
            jax.ShapeDtypeStruct((packs, packed_rows, features), bf16),
            jax.ShapeDtypeStruct((all_rows, width), i32),
            jax.ShapeDtypeStruct((packs, packed_rows, features), i32),
            jax.ShapeDtypeStruct((hidden_dev, features), bf16),
            jax.ShapeDtypeStruct((all_rows, hidden_dev), bf16),
        ],
        scratch_shapes=[
            pltpu.VMEM((all_rows, hidden_dev), bf16),
            pltpu.VMEM((all_rows, width), i32),
            pltpu.VMEM((all_rows, width), i32),
            pltpu.VMEM((hidden_dev, features), bf16),
            pltpu.VMEM((1, features), f32),
            pltpu.VMEM((hidden_dev, width), bf16),
            pltpu.VMEM((2, packs, tile, features), i32),
            pltpu.VMEM((2, packs, tile, features), bf16),
            pltpu.VMEM((shards, tile, width), f32),
            pltpu.VMEM((shards, tile, width), f32),
            pltpu.VMEM((tile, width), bf16),
            pltpu.VMEM((shards, tile, width), bf16),
            dma((5,)), dma((3,)), dma((2, 3)), dma((2, 3)),
            dma((shards,)), dma((shards,)), dma((shards,)), dma((shards,)),
            dma((2,)), dma((2,)),
            dma((shards,)), dma((shards,)), dma((shards,)), dma((shards,)),
        ],
        compiler_params=pltpu.CompilerParams(
            collective_id=1, has_side_effects=True, vmem_limit_bytes=60 * 1024 * 1024
        ),
        name="front",
    )(activations, lists, encoder_weight, decoder_weight, bias)


def body(activations, top_lists, encoder_weight, encoder_bias, decoder_weight, decoder_bias):
    group_rows, hidden_dev = activations.shape
    feat_dev = encoder_weight.shape[1]
    top = top_lists.shape[1]
    shards, groups = lax.axis_size("feat"), lax.axis_size("tok")
    owner, group = lax.axis_index("feat"), lax.axis_index("tok")
    width = feat_dev // groups
    features = shards * width
    packs = width // top
    all_rows = group_rows * groups

    bias = lax.dynamic_update_slice(
        jnp.zeros((1, features), jnp.float32),
        lax.dynamic_slice_in_dim(encoder_bias, group * width, width)[None, :],
        (0, owner * width),
    )
    lists = lax.dynamic_update_slice(
        jnp.full((group_rows, width), -1, jnp.int32), top_lists, (0, group // (groups // packs) * top)
    )
    codes, ids, places, decoder_own, inputs = front(
        shards, groups, packs, top, activations, lists, encoder_weight, decoder_weight, bias
    )
    packed_ids = ids.reshape(packs, all_rows // packs, width)
    codes = codes.reshape(all_rows, features)
    rebuilt = lax.psum_scatter(
        lax.dot_general(
            codes, decoder_own, (((1,), (1,)), ((), ())), preferred_element_type=jnp.float32
        ).astype(jnp.bfloat16),
        "tok",
        scatter_dimension=0,
        tiled=True,
    )
    own_bias = lax.dynamic_slice_in_dim(decoder_bias, owner * hidden_dev, hidden_dev)
    error_rows = (
        rebuilt.astype(jnp.float32) + own_bias - activations.astype(jnp.float32)
    ).astype(jnp.bfloat16)
    error = lax.all_gather(error_rows, "tok", axis=0, tiled=True)

    decoder_grad, encoder_grad = tail(
        shards, groups, error, inputs, codes, decoder_own, packed_ids, places
    )
    return encoder_grad.astype(jnp.float32), decoder_grad.astype(jnp.float32)


def solution(mesh):
    return jax.shard_map(
        body,
        mesh=mesh,
        in_specs=(
            P("tok", "feat"),
            P("tok", None),
            P(None, "feat"),
            P("feat"),
            P(None, "feat"),
            P(),
        ),
        out_specs=(P("tok", "feat"), P("tok", "feat")),
        check_vma=False,
    )
```
